256 devices in a mesh: grp: 4 (over x), dev: 64 (over y, z, core).
Axes of the slice: x: 4, y: 4, z: 8, core: 2. Of those that a mesh axis runs over, the one named last changes fastest.
Arguments:
- embeds: bfloat16 [24576, 1024], P(('grp', 'dev')), may hold values from -6 to 6
- cluster: int32 [24576], P(('grp', 'dev')), may hold values from 0 to 7, as said below
- priority: int32 [24576], P(('grp', 'dev')), may hold values from 0 to 24575, each once
Outputs:
- best: float32 [24576], P(('grp', 'dev'))
The draws below stay inside these ranges and needn't reach their ends.
Inputs may be any that keep to these rules, and one draw needn't show every extreme that they name: `cluster`: cluster c belongs to group c // 2. Among the items of one device, at most 48 belong to the clusters of one group, and exactly 48 to some group. `priority`: each number appears once.
All inputs are finite; a program needn't handle non-finite values.
Results may differ from the reference program's by a relative error of at most 0.0013.
Values may be sent and summed in bfloat16 or wider, within the bound.
No kernel may reach another device: no remote copies, remote signals or barrier semaphores. Data moves between devices by JAX's collectives and lax.ppermute only.
A program may use at most 128 MiB of HBM per device.

```python
import jax
import jax.numpy as jnp
from jax import lax

D = 1024
ITEM_DEV = 96
CLUST_GRP = 2
CAP = 48
ITEMS = 24576
N_GRP = 4
DEVICES = 256


def draw_cluster(key, part):
    subkeys = jax.random.split(key, 6)
    primary = jnp.minimum(jax.random.randint(subkeys[0], (DEVICES,), 0, N_GRP), jax.random.randint(subkeys[1], (DEVICES,), 0, N_GRP))
    offsets = jax.random.randint(subkeys[2], (DEVICES, ITEM_DEV - CAP), 1, N_GRP)
    others = (primary[:, None] + offsets) % N_GRP
    group_of = jnp.concatenate([jnp.broadcast_to(primary[:, None], (DEVICES, CAP)), others], axis=1)
    noise = jax.random.randint(subkeys[3], (DEVICES, ITEM_DEV), 0, 2 ** 20) * ITEM_DEV + jnp.arange(ITEM_DEV, dtype=jnp.int32)[None, :]
    shuffle = jnp.argsort(noise, axis=1, stable=True)
    group_of = jnp.take_along_axis(group_of, shuffle, axis=1)
    within = jnp.minimum(jax.random.randint(subkeys[4], (DEVICES, ITEM_DEV), 0, CLUST_GRP), jax.random.randint(subkeys[5], (DEVICES, ITEM_DEV), 0, CLUST_GRP))
    return (group_of * CLUST_GRP + within).reshape(-1).astype(jnp.int32)


def level_of(rng, dims, cuts, least, largest):
    def one(dim, parts):
        draws = jax.random.uniform(jax.random.fold_in(jax.random.fold_in(rng, 6), dim), (parts,), jnp.float32, least / len(cuts), largest / len(cuts))
        return jnp.repeat(jnp.exp(draws), dims[dim] // parts).reshape((-1,) + (1,) * (len(dims) - dim - 1))

    loudness = one(*cuts[0])
    for cut in cuts[1:]:
        loudness = loudness * one(*cut)
    return loudness


def bell_draw(stream_key, extent, width, bound, cuts=(), kind=jnp.bfloat16):
    level = level_of(stream_key, extent, cuts, -0.22, 0.18) if cuts else 1.0
    drawn = jax.random.normal(stream_key, extent, jnp.float32) * width * level
    return jnp.minimum(jnp.maximum(drawn, -bound), bound).astype(kind)


def setup_inputs(seed: int = 0) -> dict:
    splits = jax.random.split(jax.random.key(seed), 4)
    embeds = bell_draw(splits[0], (ITEMS, D), 1.0, 6.0, ((0, 256),))
    cluster = draw_cluster(jax.random.fold_in(splits[3], 71), 0)
    priority = jax.random.permutation(splits[2], ITEMS).astype(jnp.int32)
    return {"embeds": embeds, "cluster": cluster, "priority": priority}


def reference(embeds, cluster, priority):
    values = embeds.astype(jnp.float32)
    normed = (values * lax.rsqrt(lax.optimization_barrier(jnp.sum(values * values, axis=1, keepdims=True)) + 1e-06)).astype(jnp.bfloat16)
    block_rows = ITEM_DEV * 8

    def one_block(pieces):
        left, left_cluster, left_rank = pieces
        scores = jnp.dot(left, normed.T, preferred_element_type=jnp.float32)
        chosen = (left_cluster[:, None] == cluster[None, :]) & (priority[None, :] < left_rank[:, None])
        return lax.optimization_barrier(jnp.max(jnp.where(chosen, scores, -1.0), axis=1))
    result = lax.map(one_block, (normed.reshape(-1, block_rows, D), cluster.reshape(-1, block_rows), priority.reshape(-1, block_rows)))
    return result.reshape(-1)
```

```python
import jax
import jax.numpy as jnp
from jax import lax
from jax.experimental import pallas as pl
from jax.experimental.pallas import tpu as pltpu
from jax.sharding import PartitionSpec as P

ITEM = 96
ROWS = 104
D = 1024
SX, SY, SZ, SC = 4, 4, 8, 2
BASE = 256.0
RANKS = 24576.0
AXES = ("grp", "dev")


def chip_shift(delta0, delta1):
    pairs = []
    for x in range(SX):
        for y in range(SY):
            for z in range(SZ):
                for c in range(SC):
                    dx, dy, dz = (delta0, delta1)[c]
                    to = (
                        (((x + dx) % SX) * SY + (y + dy) % SY) * SZ + (z + dz) % SZ
                    ) * SC + c
                    pairs.append((((x * SY + y) * SZ + z) * SC + c, to))
    return pairs


def move(v, axis, sign=1):
    d = [0, 0, 0]
    d[axis] = sign
    return lax.ppermute(v, AXES, chip_shift(tuple(d), tuple(-e for e in d)))


def swap(v):
    n = SX * SY * SZ * SC
    return lax.ppermute(v, AXES, [(i, i ^ 1) for i in range(n)])


def pack_kernel(e_ref, c_ref, p_ref, o_ref):
    v = e_ref[...].astype(jnp.float32)
    s = jnp.sum(v * v, axis=1, keepdims=True)
    o_ref[0:ITEM, :] = (v * lax.rsqrt(s + 1e-06)).astype(jnp.bfloat16)
    c = c_ref[...]
    p = p_ref[...]
    hi = p // 256
    lo = p - hi * 256
    r = lax.broadcasted_iota(jnp.int32, (8, 128), 0)
    d = jnp.where(r == 0, c, jnp.where(r == 1, hi, lo)).astype(jnp.float32)
    o_ref[ITEM:ROWS, 0:128] = d.astype(jnp.bfloat16)
    o_ref[ITEM:ROWS, 128:] = jnp.zeros((8, D - 128), jnp.bfloat16)


def pack(embeds, cluster, priority):
    fill = ((0, 0), (0, 128 - ITEM))
    c = jnp.pad(cluster[None, :], fill, constant_values=-1)
    p = jnp.pad(priority[None, :], fill, constant_values=0)
    return pl.pallas_call(
        pack_kernel,
        out_shape=jax.ShapeDtypeStruct((ROWS, D), jnp.bfloat16),
    )(embeds, c, p)


def digits(ref, at):
    d = ref[at : at + 8, 0:128].astype(jnp.float32)
    low = d[0:1] * RANKS
    return low, low + d[1:2] * BASE + d[2:3]


def pair_kernel(pos_ref, r_ref, c_ref, o_ref, acc, key, low):
    step = pl.program_id(0)

    @pl.when(step == 0)
    def _():
        acc[...] = jnp.full_like(acc, -1.0)
        for b in range(16):
            lo, k = digits(r_ref, b * ROWS + ITEM)
            low[0:1, b * ROWS : (b + 1) * ROWS] = lo[:, :ROWS]
            key[0:1, b * ROWS : (b + 1) * ROWS] = k[:, :ROWS]

    cols = []
    for h in range(2):
        _, k = digits(c_ref, h * ROWS + ITEM)
        cols.append(jnp.transpose(jnp.broadcast_to(k, (128, 128)))[:ROWS, 0:1])
    ck = jnp.concatenate(cols, axis=0)
    for n in range(8):
        at = n * 2 * ROWS
        s = lax.dot_general(
            c_ref[...],
            r_ref[at : at + 2 * ROWS, :],
            (((1,), (1,)), ((), ())),
            preferred_element_type=jnp.float32,
        )
        ok = (ck >= low[0:1, at : at + 2 * ROWS]) & (ck < key[0:1, at : at + 2 * ROWS])
        m = jnp.max(jnp.where(ok, s, -1.0), axis=0, keepdims=True)
        acc[0:1, at : at + 2 * ROWS] = jnp.maximum(acc[0:1, at : at + 2 * ROWS], m)

    @pl.when(step == pl.num_programs(0) - 1)
    def _():
        z = pos_ref[0]
        sign = 1 - 2 * pos_ref[1]
        for b in range(16):
            off, kind = SOURCES[b]
            to = lax.rem(z + sign * off + 2 * SZ, SZ)
            v = acc[0:1, b * ROWS : b * ROWS + ITEM]
            o_ref[pl.ds(to * 2 + kind, 1), 0:ITEM] = v
            o_ref[pl.ds(to * 2 + kind, 1), ITEM:] = jnp.zeros((1, 128 - ITEM), jnp.float32)


SOURCES = (
    [(0, 0), (0, 1)]
    + [(-k, h) for k in (1, 2, 3) for h in (0, 1)]
    + [(k, 1 - h) for k in (1, 2, 3) for h in (0, 1)]
    + [(-4, 0), (-4, 1)]
)


def pairs(pos, rows, cols):
    return pl.pallas_call(
        pair_kernel,
        grid_spec=pltpu.PrefetchScalarGridSpec(
            num_scalar_prefetch=1,
            grid=(8,),
            in_specs=[
                pl.BlockSpec((16 * ROWS, D), lambda i, p: (0, 0)),
                pl.BlockSpec((2 * ROWS, D), lambda i, p: (i, 0)),
            ],
            out_specs=pl.BlockSpec((16, 128), lambda i, p: (0, 0)),
            scratch_shapes=[
                pltpu.VMEM((1, 16 * ROWS), jnp.float32),
                pltpu.VMEM((1, 16 * ROWS), jnp.float32),
                pltpu.VMEM((1, 16 * ROWS), jnp.float32),
            ],
        ),
        out_shape=jax.ShapeDtypeStruct((16, 128), jnp.float32),
    )(pos, rows, cols)


def per_device(embeds, cluster, priority):
    dev = lax.axis_index("dev")
    pos = jnp.stack([(dev // SC) % SZ, dev % SC]).astype(jnp.int32)
    own = pack(embeds, cluster, priority)
    chip = jnp.concatenate([own, swap(own)], axis=0)
    a1, x1, y1 = move(chip, 2), move(chip, 0), move(chip, 1)
    a2, x2, y2 = move(a1, 2), move(y1, 0), move(x1, 1, -1)
    a3 = move(a2, 2)
    x3 = move(jnp.concatenate([x2, x1[:ROWS]], axis=0), 0)
    y3 = move(jnp.concatenate([x2, y1[:ROWS]], axis=0), 1)
    a4 = move(a3[:ROWS], 2)
    x4 = move(y3[:ROWS], 0)
    s1, s2, s3, s4 = swap(a1), swap(a2), swap(a3), swap(a4)
    rows = jnp.concatenate([chip, a1, a2, a3, s1, s2, s3, a4, s4], axis=0)
    cols = jnp.concatenate([own, x1, y1, x2, y2, x3, y3, x4], axis=0)
    best = pairs(pos, rows, cols)
    groups = [
        [(y * SZ + z) * SC + c for z in range(SZ)] for y in range(SY) for c in range(SC)
    ]
    back = lax.all_to_all(
        best.reshape(SZ, 2, 128), "dev", split_axis=0, concat_axis=0, axis_index_groups=groups
    )
    part = jnp.max(back.reshape(SZ, 2, 128), axis=0)
    return jnp.maximum(part[0], swap(part[1]))[:ITEM]


def solution(mesh):
    in_specs = (P(AXES, None), P(AXES), P(AXES))
    return jax.shard_map(
        per_device, mesh=mesh, in_specs=in_specs, out_specs=P(AXES), check_vma=False
    )
```

```python
import functools

import jax
import jax.numpy as jnp
from jax import lax
from jax.experimental import pallas as pl
from jax.experimental.pallas import tpu as pltpu
from jax.sharding import PartitionSpec as P

ITEM = 96
HALF = 104
CHIP = 200
D = 1024
SX, SY, SZ, SC = 4, 4, 8, 2
BASE = 256.0
RANKS = 24576.0
AXES = ("grp", "dev")
VMEM = pl.BlockSpec(memory_space=pltpu.VMEM)


def shift(v, delta):
    pairs = []
    for x in range(SX):
        for y in range(SY):
            for z in range(SZ):
                for c in range(SC):
                    dx, dy, dz = (e if c == 0 else -e for e in delta)
                    to = (((x + dx) % SX) * SY + (y + dy) % SY) * SZ + (z + dz) % SZ
                    pairs.append((((x * SY + y) * SZ + z) * SC + c, to * SC + c))
    return lax.ppermute(v, AXES, pairs)


def swap(v):
    return lax.ppermute(v, AXES, [(i, i ^ 1) for i in range(SX * SY * SZ * SC)])


def call(kernel, out_shape, *args, limit=16 << 20, flops=0, specs=None):
    return pl.pallas_call(
        kernel,
        out_shape=out_shape,
        in_specs=specs or [VMEM] * len(args),
        out_specs=jax.tree.map(lambda _: VMEM, out_shape),
        compiler_params=pltpu.CompilerParams(vmem_limit_bytes=limit),
        cost_estimate=pl.CostEstimate(flops=flops, bytes_accessed=1 << 16, transcendentals=0),
    )(*args)


def pack_kernel(e_ref, c_ref, p_ref, o_ref):
    v = e_ref[...].astype(jnp.float32)
    s = jnp.sum(v * v, axis=1, keepdims=True)
    o_ref[0:ITEM, :] = (v * lax.rsqrt(s + 1e-06)).astype(jnp.bfloat16)
    c, p = c_ref[...], p_ref[...]
    r = lax.broadcasted_iota(jnp.int32, (8, ITEM), 0)
    d = jnp.where(r == 0, c, jnp.where(r == 1, p >> 8, p & 255)).astype(jnp.float32)
    o_ref[ITEM:HALF, :] = jnp.zeros((8, D), jnp.bfloat16)
    o_ref[ITEM:HALF, 0:ITEM] = d.astype(jnp.bfloat16)


def join_kernel(a_ref, b_ref, o_ref):
    o_ref[0:ITEM, :] = a_ref[0:ITEM, :]
    o_ref[ITEM : 2 * ITEM, :] = b_ref[0:ITEM, :]
    o_ref[2 * ITEM : CHIP, 0:128] = a_ref[ITEM:HALF, 0:128]
    o_ref[2 * ITEM : CHIP, 128:256] = b_ref[ITEM:HALF, 0:128]
    o_ref[2 * ITEM : CHIP, 256:] = jnp.zeros((8, D - 256), jnp.bfloat16)


def half(chip):
    return jnp.concatenate([chip[:ITEM], chip[2 * ITEM :]], axis=0)


def chip_at(i, base=0, flip=False):
    a, b = (i, base, base + 192, 0), (i, base + ITEM, base + 192, 128)
    return [b, a] if flip else [a, b]


def half_at(i, base=0):
    return [(i, base, base + ITEM, 0)]


def digits(refs, h):
    i, _, row, lane = h
    d = refs[i][row : row + 8, lane : lane + 128].astype(jnp.float32)
    low = d[0:1] * RANKS
    return low, low + d[1:2] * BASE + d[2:3]


def items(refs, halves):
    return jnp.concatenate([refs[h[0]][h[1] : h[1] + ITEM, :] for h in halves], axis=0)


def pieces(n, most):
    k = -(-n // most)
    cut = [(n * j // k) for j in range(k + 1)]
    return list(zip(cut[:-1], cut[1:]))


def sweep(refs, rows, cols):
    lows, keys = zip(*[digits(refs, h) for h in rows])
    low = jnp.concatenate([v[:, :ITEM] for v in lows], axis=1)
    key = jnp.concatenate([v[:, :ITEM] for v in keys], axis=1)
    n = len(rows) * ITEM
    best = [None] * (-(-n // 512))
    for a, b in pieces(len(cols), 6):
        c = items(refs, cols[a:b])
        ck = jnp.concatenate(
            [
                jnp.transpose(jnp.broadcast_to(digits(refs, h)[1], (128, 128)))[:ITEM]
                for h in cols[a:b]
            ],
            axis=0,
        )
        r = items(refs, rows)
        for j in range(len(best)):
            lo, hi = j * 512, min(n, j * 512 + 512)
            s = lax.dot_general(
                c, r[lo:hi], (((1,), (1,)), ((), ())), preferred_element_type=jnp.float32
            )
            k = jnp.concatenate([ck] * (-(-(hi - lo) // 128)), axis=1)[:, : hi - lo]
            ok = (k >= low[:, lo:hi]) & (k < key[:, lo:hi])
            m = jnp.max(jnp.where(ok, s, -1.0), axis=0, keepdims=True)
            best[j] = m if best[j] is None else jnp.maximum(best[j], m)
    return jnp.concatenate(best, axis=1) if len(best) > 1 else best[0]


def stage_kernel(plan, n_data, n_acc, *refs):
    data, accs, outs = refs[:n_data], refs[n_data : n_data + n_acc], refs[n_data + n_acc :]
    for rows, cols, old, widths, to in plan:
        m = sweep(data, rows, cols)
        at = 0
        for w, o, t in zip(widths, old, to):
            v = m[:, at : at + w]
            outs[t][...] = v if o is None else jnp.maximum(accs[o][...], v)
            at += w


def stage(plan, data, accs, n_out_widths):
    flops = sum(2 * len(r) * len(c) * ITEM * ITEM * D for r, c, *_ in plan)
    return call(
        functools.partial(stage_kernel, plan, len(data), len(accs)),
        [jax.ShapeDtypeStruct((1, w), jnp.float32) for w in n_out_widths],
        *data,
        *accs,
        flops=flops,
    )


HOMES = (0, -1, 1, -2, 2, -3, 3, -4)


def last_kernel(rows, cols, n_data, *refs):
    pos_ref, data, (g1, g2, g3, o_ref) = refs[0], refs[1 : 1 + n_data], refs[1 + n_data :]
    g4 = sweep(data, rows, cols)
    dev = pos_ref[0]
    z = lax.rem(dev // SC, SZ)
    sign = 1 - 2 * lax.rem(dev, SC)
    o_ref[...] = jnp.full_like(o_ref, -1.0)
    at = 0
    parts = [(g1[...], 3), (g2[...], 2), (g3[...], 2), (g4, 1)]
    chip = 0
    for v, n in parts:
        for j in range(n):
            to = lax.rem(z + sign * HOMES[chip] + 2 * SZ, SZ)
            for kind in range(2):
                b = (2 * j + kind) * ITEM
                o_ref[pl.ds(to * 2 + kind, 1), 0:ITEM] = v[:, b : b + ITEM]
            chip += 1


def per_device(embeds, cluster, priority):
    pos = lax.axis_index("dev").astype(jnp.int32).reshape(1)
    shape = functools.partial(jax.ShapeDtypeStruct, dtype=jnp.bfloat16)
    own = call(
        pack_kernel, shape((HALF, D)), embeds, cluster.reshape(1, ITEM), priority.reshape(1, ITEM),
        limit=4 << 20,
    )
    chip = call(join_kernel, shape((CHIP, D)), own, swap(own), limit=4 << 20)
    a1, x1, y1 = shift(chip, (0, 0, 1)), shift(chip, (1, 0, 0)), shift(chip, (0, 1, 0))
    s1 = swap(a1)
    a2, x2, y2 = shift(a1, (0, 0, 1)), shift(y1, (1, 0, 0)), shift(x1, (0, -1, 0))
    s2 = swap(a2)
    a3 = shift(a2, (0, 0, 1))
    s3 = swap(a3)
    x3 = shift(jnp.concatenate([x2, half(x1)], axis=0), (1, 0, 0))
    y3 = shift(jnp.concatenate([x2, half(y1)], axis=0), (0, 1, 0))
    d3 = shift(half(x2), (1, 1, 0))
    a4 = shift(half(a3), (0, 0, 1))
    s4 = swap(a4)

    (g1,) = stage(
        [(
            chip_at(0) + chip_at(1) + chip_at(2, flip=True),
            chip_at(0)[:1] + chip_at(3) + chip_at(4),
            [None], [576], [0],
        )],
        [chip, a1, s1, x1, y1], [], [576],
    )
    data = [chip, a1, s1, x1, y1, a2, s2, x2, y2]
    r1 = chip_at(0) + chip_at(1) + chip_at(2, flip=True)
    r2 = chip_at(5) + chip_at(6, flip=True)
    c1 = chip_at(0)[:1] + chip_at(3) + chip_at(4)
    c2 = chip_at(7) + chip_at(8)
    g1, g2 = stage(
        [(r1, c2, [0], [576], [0]), (r2, c1 + c2, [None], [384], [1])], data, [g1], [576, 384]
    )
    data = data + [a3, s3, x3, y3, d3]
    r3 = chip_at(9) + chip_at(10, flip=True)
    c3 = (
        chip_at(11) + half_at(11, CHIP) + chip_at(12) + half_at(12, CHIP) + half_at(13)
    )
    g1, g2, g3 = stage(
        [
            (r1 + r2, c3, [0, 1], [576, 384], [0, 1]),
            (r3, c1 + c2 + c3, [None], [384], [2]),
        ],
        data, [g1, g2], [576, 384, 384],
    )
    data = [chip, x1, y1, x2, y2, x3, y3, d3, a4, s4]
    cols = (
        chip_at(0)[:1] + chip_at(1) + chip_at(2) + chip_at(3) + chip_at(4)
        + chip_at(5) + half_at(5, CHIP) + chip_at(6) + half_at(6, CHIP) + half_at(7)
    )
    best = call(
        functools.partial(last_kernel, half_at(8) + half_at(9), cols, len(data)),
        jax.ShapeDtypeStruct((2 * SZ, 128), jnp.float32),
        pos, *data, g1, g2, g3,
        flops=2 * 2 * ITEM * 1536 * D,
        specs=[pl.BlockSpec(memory_space=pltpu.SMEM)] + [VMEM] * (len(data) + 3),
    )
    groups = [[(y * SZ + z) * SC + c for z in range(SZ)] for y in range(SY) for c in range(SC)]
    back = lax.all_to_all(
        best.reshape(SZ, 2, 128), "dev", split_axis=0, concat_axis=0, axis_index_groups=groups
    )
    part = jnp.max(back.reshape(SZ, 2, 128), axis=0)
    return jnp.maximum(part[0], swap(part[1]))[:ITEM]


def solution(mesh):
    in_specs = (P(AXES, None), P(AXES), P(AXES))
    return jax.shard_map(
        per_device, mesh=mesh, in_specs=in_specs, out_specs=P(AXES), check_vma=False
    )
```
